512 devices in a mesh: gx: 8 (over y, core), gy: 4 (over x), gz: 16 (over z).
Axes of the slice: x: 4, y: 4, z: 16, core: 2. Of those that a mesh axis runs over, the one named last changes fastest.
Arguments:
- level_set: float32 [128, 64, 2048], P('gx', 'gy', 'gz'), may hold values from 0 to 1
- velocity: float32 [3, 128, 64, 2048], P(None, 'gx', 'gy', 'gz'), may hold values from -6 to 6
- source: float32 [128, 64, 2048], P('gx', 'gy', 'gz'), may hold values from -6 to 6
- coarse_factor: float32 [512, 512], P(('gx', 'gy', 'gz')), may hold values from -0.2 to 0.2
Outputs:
- level_set_new: float32 [128, 64, 2048], P('gx', 'gy', 'gz')
- pressure: float32 [128, 64, 2048], P('gx', 'gy', 'gz')
The draws below stay inside these ranges and needn't reach their ends.
All inputs are finite; a program needn't handle non-finite values.
Results may differ from the reference program's by a relative error of at most 0.029.
Values sent between devices are 32-bit elements; how exact they have to be, the bound alone decides.
A program may use at most 64 MiB of HBM per device.

```python
import math
import jax
import jax.numpy as jnp
import numpy as np
from jax import lax

NP = 8
ELX = 2
ELY = 2
ELZ = 16
RSWEEPS = 2
ITERS = 6
NX = 128
NY = 64
NZ = 2048
NCOARSE = 512
N_GX = 8
N_GY = 4
N_GZ = 16


def draw_coarse_factor(key, part):
    first_key = jax.random.fold_in(key, 11)
    second_key = jax.random.fold_in(key, 23)
    noise = jax.random.normal(first_key, (NCOARSE, NCOARSE), jnp.float32)
    leading = jax.random.uniform(second_key, (NCOARSE,), jnp.float32, 0.6, 1.4)
    return 0.05 * (jnp.diag(leading) + 0.6 * noise / math.sqrt(NCOARSE))


def block_scale(stream_key, extent, pieces, low, top_value):
    def one(dim, shards_of):
        heights = jax.random.uniform(jax.random.fold_in(jax.random.fold_in(stream_key, 6), dim), (shards_of,), jnp.float32, low / len(pieces), top_value / len(pieces))
        return jnp.repeat(jnp.exp(heights), extent[dim] // shards_of).reshape((-1,) + (1,) * (len(extent) - dim - 1))

    gain = one(*pieces[0])
    for cut in pieces[1:]:
        gain = gain * one(*cut)
    return gain


def normal_values(rng, dims, deviation, reach, pieces=(), dtype=jnp.bfloat16):
    values = jax.random.normal(rng, dims, jnp.float32) * deviation
    if len(pieces) > 0:
        values = block_scale(rng, dims, pieces, -0.22, 0.18) * values
    return jnp.clip(values, min=-reach, max=reach).astype(dtype)


def setup_inputs(seed: int = 0) -> dict:
    arg_keys = jax.random.split(jax.random.key(seed), 5)
    level_set = jnp.clip(1.0 * jax.random.uniform(arg_keys[0], (NX, NY, NZ), jnp.float32) ** block_scale(arg_keys[0], (NX, NY, NZ), ((0, 8), (1, 4), (2, 16)), -0.2, 0.2), 0.0, 1.0)
    velocity = normal_values(arg_keys[1], (3, NX, NY, NZ), 1.0, 6.0, ((1, 8), (2, 4), (3, 16)), jnp.float32)
    source = normal_values(arg_keys[2], (NX, NY, NZ), 1.0, 6.0, ((0, 8), (1, 4), (2, 16)), jnp.float32)
    coarse_factor = draw_coarse_factor(jax.random.fold_in(arg_keys[4], 71), 0)
    return dict(level_set=level_set, velocity=velocity, source=source, coarse_factor=coarse_factor)


GLL_POINTS = (-1.0, -0.8717401485096066, -0.5917001814331423, -0.2092992179024789, 0.2092992179024789, 0.5917001814331423, 0.8717401485096066, 1.0)
GLL_WEIGHTS = (0.03571428571428571, 0.21070422714350603, 0.3411226924835044, 0.4124587946587038, 0.4124587946587038, 0.3411226924835044, 0.21070422714350603, 0.03571428571428571)
HIGHEST = lax.Precision.HIGHEST
TIME_STEP = 0.02
PSEUDO_STEP = 0.004
INTERFACE_WIDTH = 0.5
GAS_DENSITY = 0.1
SOURCE_SCALE = 20.0

def node_tables():
    points = np.array(GLL_POINTS)
    amount = points.shape[0]
    barycentric = np.ones(amount)
    for target in range(amount):
        for partner in range(amount):
            if partner != target:
                barycentric[target] = barycentric[target] / (points[target] - points[partner])
    derivative = np.zeros((amount, amount))
    for target in range(amount):
        for partner in range(amount):
            if partner != target:
                derivative[target, partner] = barycentric[partner] / barycentric[target] / (points[target] - points[partner])
        derivative[target, target] = -np.sum(derivative[target])
    return derivative

def apply_axis(values, matrix, which_axis):
    first_size, second_size, third_size = values.shape
    if which_axis == 0:
        blocks = values.reshape(first_size // NP, NP, second_size, third_size)
        result = jnp.einsum('ai,eiyz->eayz', matrix, blocks, precision=HIGHEST)
    elif which_axis == 1:
        blocks = values.reshape(first_size, second_size // NP, NP, third_size)
        result = jnp.einsum('aj,xejz->xeaz', matrix, blocks, precision=HIGHEST)
    else:
        blocks = values.reshape(first_size, second_size, third_size // NP, NP)
        result = jnp.einsum('ak,xyek->xyea', matrix, blocks, precision=HIGHEST)
    return result.reshape(values.shape)

def edge_passes(padded):
    summed = padded
    for which_axis in (1, 2, 3):
        amount = summed.shape[which_axis] - 2
        center = lax.slice_in_dim(summed, 1, amount + 1, axis=which_axis)
        upper_side = lax.slice_in_dim(summed, 2, amount + 2, axis=which_axis)
        lower_side = lax.slice_in_dim(summed, 0, amount, axis=which_axis)
        shape_list = [1, 1, 1, 1]
        shape_list[which_axis] = amount
        position = (jnp.arange(amount) % NP).reshape(shape_list)
        summed = center + jnp.where(position == NP - 1, upper_side, 0.0) + jnp.where(position == 0, lower_side, 0.0)
    return summed

def assemble(stacked):
    return edge_passes(jnp.pad(stacked, ((0, 0), (1, 1), (1, 1), (1, 1))))

def mass_weights(shape_tuple):
    weights = jnp.asarray(np.array(GLL_WEIGHTS), jnp.float32)
    along_x = jnp.tile(weights, shape_tuple[0] // NP)
    along_y = jnp.tile(weights, shape_tuple[1] // NP)
    along_z = jnp.tile(weights, shape_tuple[2] // NP)
    return along_x[:, None, None] * along_y[None, :, None] * along_z[None, None, :]

def reference(level_set, velocity, source, coarse_factor):
    derivative = node_tables()
    deriv_table = jnp.asarray(derivative, jnp.float32)
    deriv_trans = jnp.asarray(derivative.T, jnp.float32)
    square_trans = jnp.asarray((derivative * derivative).T, jnp.float32)
    bmass = mass_weights(level_set.shape)
    gradient = [apply_axis(level_set, deriv_table, which_axis) for which_axis in range(3)]
    advect = velocity[0] * gradient[0] + velocity[1] * gradient[1] + velocity[2] * gradient[2]
    divergence = apply_axis(bmass * velocity[0], deriv_trans, 0) + apply_axis(bmass * velocity[1], deriv_trans, 1) + apply_axis(bmass * velocity[2], deriv_trans, 2) + bmass * source
    assembled = assemble(jnp.stack([bmass * advect, bmass, divergence]))
    mass_sum = assembled[1]
    weight = bmass / mass_sum
    level_now = level_set - TIME_STEP * assembled[0] / mass_sum
    rhs_field = SOURCE_SCALE * assembled[2]
    for sweep in range(RSWEEPS):
        gradient = [apply_axis(level_now, deriv_table, which_axis) for which_axis in range(3)]
        inv_norm = 1.0 / jnp.sqrt(1.0 + gradient[0] * gradient[0] + gradient[1] * gradient[1] + gradient[2] * gradient[2])
        compress = level_now * (1.0 - level_now) * inv_norm
        weak_form = apply_axis(bmass * (compress * gradient[0] - INTERFACE_WIDTH * gradient[0]), deriv_trans, 0)
        weak_form = weak_form + apply_axis(bmass * (compress * gradient[1] - INTERFACE_WIDTH * gradient[1]), deriv_trans, 1)
        weak_form = weak_form + apply_axis(bmass * (compress * gradient[2] - INTERFACE_WIDTH * gradient[2]), deriv_trans, 2)
        level_now = level_now + PSEUDO_STEP * assemble(weak_form[None])[0] / mass_sum
    inverse_density = 1.0 / (GAS_DENSITY + (1.0 - GAS_DENSITY) * jnp.clip(level_now, 0.0, 1.0))
    scaled = bmass * inverse_density
    diag_local = apply_axis(scaled, square_trans, 0) + apply_axis(scaled, square_trans, 1) + apply_axis(scaled, square_trans, 2) + bmass
    diagonal = assemble(diag_local[None])[0]

    def operator(values):
        local_part = bmass * values
        for which_axis in range(3):
            local_part = local_part + apply_axis(scaled * apply_axis(values, deriv_table, which_axis), deriv_trans, which_axis)
        return assemble(local_part[None])[0]

    def precondition(residual):
        blocked = (weight * residual).reshape(N_GX, ELX * NP, N_GY, ELY * NP, N_GZ, ELZ * NP)
        restricted = lax.optimization_barrier(jnp.sum(blocked, axis=(1, 3, 5))).reshape(-1)
        coarse_mid = jnp.dot(coarse_factor.T, restricted, precision=HIGHEST)
        coarse_value = jnp.dot(coarse_factor, coarse_mid, precision=HIGHEST).reshape(N_GX, 1, N_GY, 1, N_GZ, 1)
        spread = (weight.reshape(N_GX, ELX * NP, N_GY, ELY * NP, N_GZ, ELZ * NP) * coarse_value).reshape(weight.shape)
        result = residual / diagonal + assemble(spread[None])[0]
        return (result, jnp.sum(weight * residual * result))
    pressure = jnp.zeros_like(rhs_field)
    residual = rhs_field
    direction, inner_now = precondition(residual)
    for step in range(ITERS):
        image = operator(direction)
        step_size = inner_now / jnp.sum(weight * direction * image)
        pressure = pressure + step_size * direction
        residual = residual - step_size * image
        if step + 1 < ITERS:
            preconditioned, inner_next = precondition(residual)
            direction = preconditioned + inner_next / inner_now * direction
            inner_now = inner_next
    return (level_now, pressure)
```

```python
import functools

import jax
import jax.numpy as jnp
import numpy as np
from jax import lax
from jax.experimental import pallas as pl
from jax.experimental.pallas import tpu as pltpu
from jax.sharding import PartitionSpec as P

NP = 8
RSWEEPS = 2
ITERS = 6

GLL_POINTS = (
    -1.0,
    -0.8717401485096066,
    -0.5917001814331423,
    -0.2092992179024789,
    0.2092992179024789,
    0.5917001814331423,
    0.8717401485096066,
    1.0,
)
GLL_WEIGHTS = (
    0.03571428571428571,
    0.21070422714350603,
    0.3411226924835044,
    0.4124587946587038,
    0.4124587946587038,
    0.3411226924835044,
    0.21070422714350603,
    0.03571428571428571,
)
HIGHEST = lax.Precision.HIGHEST
TIME_STEP = 0.02
PSEUDO_STEP = 0.004
INTERFACE_WIDTH = 0.5
GAS_DENSITY = 0.1
SOURCE_SCALE = 20.0
MESH = pl.DeviceIdType.MESH
AXES = ("gx", "gy", "gz")
LANES = 128
OFFSETS = tuple(
    (i, j, k) for i in (-1, 0, 1) for j in (-1, 0, 1) for k in (-1, 0, 1) if (i, j, k) != (0, 0, 0)
)


def node_tables():
    points = np.array(GLL_POINTS)
    amount = points.shape[0]
    barycentric = np.ones(amount)
    for target in range(amount):
        for partner in range(amount):
            if partner != target:
                barycentric[target] = barycentric[target] / (points[target] - points[partner])
    derivative = np.zeros((amount, amount))
    for target in range(amount):
        for partner in range(amount):
            if partner != target:
                derivative[target, partner] = (
                    barycentric[partner] / barycentric[target] / (points[target] - points[partner])
                )
        derivative[target, target] = -np.sum(derivative[target])
    return derivative


def two_parts(matrix):
    matrix = matrix.astype(np.float32)
    high = matrix.astype(jnp.bfloat16)
    low = (matrix - high.astype(np.float32)).astype(jnp.bfloat16)
    return high, low


def block_tables(nx, ny, nz):
    d = node_tables()
    sq = (d * d).T

    def blocks(n, m):
        return np.kron(np.eye(n // NP), m)

    along_x = np.kron(blocks(nx, d), np.eye(ny))
    along_y = np.kron(np.eye(nx), blocks(ny, d))
    left = np.concatenate([along_x, along_y], axis=0)
    square = np.kron(blocks(nx, sq), np.eye(ny)) + np.kron(np.eye(nx), blocks(ny, sq))
    w = np.array(GLL_WEIGHTS, np.float32)
    rows = (np.tile(w, nx // NP)[:, None] * np.tile(w, ny // NP)[None, :]).reshape(-1, 1)
    mass = (rows * np.tile(w, nz // NP)[None, :]).astype(np.float32)
    tables = []
    for m in (left, left.T, blocks(nz, d.T), blocks(nz, d), square, blocks(nz, d * d)):
        tables.extend(two_parts(m))
    return tables, mass


def parts_of(value):
    high = value.astype(jnp.bfloat16)
    low = (value - high.astype(jnp.float32)).astype(jnp.bfloat16)
    return high, low


def mm(a, b):
    return jnp.dot(a, b, preferred_element_type=jnp.float32)


def left_product(high, low, parts):
    return mm(high, parts[0]) + (mm(high, parts[1]) + mm(low, parts[0]))


def right_product(parts, high, low):
    return mm(parts[0], high) + (mm(parts[1], high) + mm(parts[0], low))


def exact(a, b, ca, cb):
    return lax.dot_general(
        a, b, (((ca,), (cb,)), ((), ())), precision=HIGHEST, preferred_element_type=jnp.float32
    )


def kernel(cfg, *refs):
    sizes, nx, ny, nz, ncoarse = cfg
    sx, sy, sz = sizes
    rows = nx * ny
    crows = ncoarse // LANES
    halves = rows // LANES
    (ls, vel, src, xrow) = refs[:4]
    (lxh, lxl, lth, ltl, rzh, rzl, rth, rtl, sqh, sql, szh, szl) = refs[4:16]
    mass = refs[16]
    lev_out, p_out = refs[17:19]
    (
        qs, ysend, zsend, recvf, recvz, az, msg, arp, arz, xnb, xin, zmask, phi, wt, ibw, scaled, invd,
        rf, zf, pf, apf, mv, ends, sxy, rxy, rzs, ssa, rpa, rza, xss, xrs,
    ) = refs[19:]

    me = [lax.axis_index(a) for a in AXES]

    def device(offset):
        return tuple(
            lax.rem(me[i] + (offset[i] % sizes[i]), sizes[i]) if offset[i] % sizes[i] else me[i]
            for i in range(3)
        )

    plane_peers = [(i, j, 0) for i in range(sx) for j in range(sy) if (i, j) != (0, 0)]
    line_peers = [(0, 0, k) for k in range(1, sz)]

    has_lo = [jnp.where(me[i] > 0, 1.0, 0.0).astype(jnp.float32) for i in range(3)]
    has_hi = [jnp.where(me[i] < sizes[i] - 1, 1.0, 0.0).astype(jnp.float32) for i in range(3)]

    row = lax.broadcasted_iota(jnp.int32, (rows, 1), 0)
    lane = lax.broadcasted_iota(jnp.int32, (1, nz), 1)
    row_x, row_y = lax.shift_right_logical(row, ny.bit_length() - 1), lax.bitwise_and(row, ny - 1)

    def inverse_copies(index, extent, dim):
        inside = lax.bitwise_and(index, NP - 1)
        low = (inside == 0) & (index > 0)
        high = (inside == NP - 1) & (index < extent - 1)
        value = jnp.where(low | high, 0.5, 1.0).astype(jnp.float32)
        value = value - jnp.where(index == 0, 0.5, 0.0) * has_lo[dim]
        return value - jnp.where(index == extent - 1, 0.5, 0.0) * has_hi[dim]

    weight = inverse_copies(row_x, nx, 0) * inverse_copies(row_y, ny, 1) * inverse_copies(lane, nz, 2)
    wt[...] = weight
    ibw[...] = weight / mass[...]

    def spread_shape(index, extent, dim, which):
        at_low = jnp.where(index == 0, 0.5, 0.0) * has_lo[dim]
        at_high = jnp.where(index == extent - 1, 0.5, 0.0) * has_hi[dim]
        own = 1.0 - at_low - at_high
        return jnp.where(which == 0, at_low, jnp.where(which == 1, own, at_high))

    flat = lax.broadcasted_iota(jnp.int32, (1, rows), 1)
    flat_x = lax.shift_right_logical(flat, ny.bit_length() - 1)
    flat_y = lax.bitwise_and(flat, ny - 1)

    def split_nine(count):
        k = lax.broadcasted_iota(jnp.int32, (count, 1), 0)
        first = jnp.where(k >= 3, 1, 0) + jnp.where(k >= 6, 1, 0)
        return k, first, k - 3 * first

    k9, kx, ky = split_nine(16)
    both = spread_shape(flat_x, nx, 0, kx) * spread_shape(flat_y, ny, 1, ky)
    phi[...] = jnp.where(k9 < 9, both, 0.0)
    phi_z = [spread_shape(lane, nz, 2, jnp.full((1, nz), kz, jnp.int32)) for kz in range(3)]

    k18 = lax.broadcasted_iota(jnp.int32, (18, 1), 0)
    upper = jnp.where(k18 >= 9, 1, 0)
    k_in = k18 - 9 * upper
    zx = jnp.where(k_in >= 3, 1, 0) + jnp.where(k_in >= 6, 1, 0)
    zy = k_in - 3 * zx

    def region(index, extent, dim, which):
        at_low = jnp.where(index == 0, 1.0, 0.0) * has_lo[dim]
        at_high = jnp.where(index == extent - 1, 1.0, 0.0) * has_hi[dim]
        return jnp.where(which == 0, at_low, jnp.where(which == 1, 1.0, at_high))

    side = jnp.where(upper == 0, has_lo[2], has_hi[2])
    zmask[...] = region(flat_x, nx, 0, zx) * region(flat_y, ny, 1, zy) * side
    wide_lane = lax.broadcasted_iota(jnp.int32, (18, nz), 1)
    target = jnp.where(k18 < 9, 0, nz - 1)
    ends[...] = jnp.where(wide_lane == target, 1.0, 0.0)
    pick_row = lax.broadcasted_iota(jnp.int32, (8, nz), 0)
    pick_lane = lax.broadcasted_iota(jnp.int32, (8, nz), 1)
    pick = jnp.where(
        ((pick_row == 0) & (pick_lane == 0)) | ((pick_row == 1) & (pick_lane == nz - 1)), 1.0, 0.0
    )

    xnb[...] = jnp.zeros_like(xnb)
    for j in range(crows):
        xnb[1, 4:5, j * LANES : (j + 1) * LANES] = xrow[j : j + 1, :]
    for par in range(2):
        msg[par] = jnp.zeros_like(msg[par])
    pf[...] = jnp.zeros_like(pf)
    apf[...] = jnp.zeros_like(apf)
    mv[...] = jnp.zeros_like(mv)
    p_out[...] = jnp.zeros_like(p_out)

    barrier = pltpu.get_barrier_semaphore()
    peers = sorted(
        {tuple(o[i] % sizes[i] for i in range(3)) for o in OFFSETS}
        | set(plane_peers)
        | set(line_peers)
    )
    for o in peers:
        pl.semaphore_signal(barrier, inc=1, device_id=device(o), device_id_type=MESH)
    pl.semaphore_wait(barrier, len(peers))

    def remote(source, dest, send, recv, offset):
        return pltpu.make_async_remote_copy(
            src_ref=source,
            dst_ref=dest,
            send_sem=send,
            recv_sem=recv,
            device_id=device(offset),
            device_id_type=MESH,
        )

    def drain(ref, sem):
        pltpu.make_async_copy(ref, ref, sem).wait()

    def nine(o):
        return (1 - o[0]) * 3 + (1 - o[1])

    for o in OFFSETS:
        place = pl.ds(OFFSETS.index(o) * crows, crows)
        remote(xrow, xin.at[place, :], xss.at[0], xrs.at[0], o).start()

    face_rows = 2 * ny + 2 * nx

    def halo_start(value, slot):
        inside = lax.bitwise_and(lane, NP - 1)
        up = (inside == NP - 1) & (lane < nz - 1)
        down = (inside == 0) & (lane > 0)
        q = (
            value
            + jnp.where(up, pltpu.roll(value, nz - 1, 1), 0.0)
            + jnp.where(down, pltpu.roll(value, 1, 1), 0.0)
        )
        field = qs.at[slot]
        field[...] = q
        for e in range(NP, ny, NP):
            total = field[pl.ds(e - 1, nx, stride=ny), :] + field[pl.ds(e, nx, stride=ny), :]
            field[pl.ds(e - 1, nx, stride=ny), :] = total
            field[pl.ds(e, nx, stride=ny), :] = total
        for e in range(NP, nx, NP):
            total = field[(e - 1) * ny : e * ny, :] + field[e * ny : (e + 1) * ny, :]
            field[(e - 1) * ny : e * ny, :] = total
            field[e * ny : (e + 1) * ny, :] = total
        ysend[slot, 0] = field[pl.ds(0, nx, stride=ny), :]
        ysend[slot, 1] = field[pl.ds(ny - 1, nx, stride=ny), :]
        face = exact(pick, field[...], 1, 1)
        for dx in (-1, 0, 1):
            for dy in (-1, 0, 1):
                shift = (-ny * dx + (ny - 1) * dy) % rows
                moved = pltpu.roll(face, shift, 1) if shift else face
                place = (dx + 1) * 3 + dy + 1
                for h in range(halves):
                    part = moved[0:2, h * LANES : (h + 1) * LANES]
                    zsend[slot, place, h : h + 1, :] = part[0:1]
                    zsend[slot, place, halves + h : halves + h + 1, :] = part[1:2]
        send, recv = sxy.at[slot], rxy.at[slot]
        for o in OFFSETS:
            if o[2] != 0:
                k, hi = nine(o), 1 if o[2] > 0 else 0
                remote(
                    zsend.at[slot, k, pl.ds(hi * halves, halves), :],
                    recvz.at[slot, pl.ds((k + (0 if hi else 9)) * halves, halves), :],
                    rzs.at[slot, 0],
                    rzs.at[slot, 1],
                    o,
                ).start()
        for o in OFFSETS:
            if o[2] == 0:
                x_row = 0 if o[0] < 0 else (nx - 1) * ny
                y_row = 0 if o[1] < 0 else ny - 1
                if o[1] == 0:
                    source = qs.at[slot, pl.ds(x_row, ny), :]
                    place, count = (0 if o[0] > 0 else ny), ny
                elif o[0] == 0:
                    source = ysend.at[slot, 0 if o[1] < 0 else 1]
                    place, count = 2 * ny + (0 if o[1] > 0 else nx), nx
                else:
                    source = qs.at[slot, pl.ds(x_row + y_row, 1), :]
                    place = face_rows + (0 if o[0] > 0 else 2) + (0 if o[1] > 0 else 1)
                    count = 1
                remote(source, recvf.at[slot, pl.ds(place, count), :], send, recv, o).start()

    def halo_finish(slot):
        drain(recvf.at[slot], rxy.at[slot])
        drain(recvz.at[slot], rzs.at[slot, 1])
        for h in range(halves):
            piece = slice(h * LANES, (h + 1) * LANES)
            arrived = recvz[slot, pl.ds(h, 18, stride=halves), :] * zmask[:, piece]
            az[piece, :] = qs[slot, piece, :] + exact(arrived, ends[...], 0, 0)
        faces = recvf.at[slot]
        az[0:ny, :] += faces[0:ny, :] * has_lo[0]
        az[rows - ny : rows, :] += faces[ny : 2 * ny, :] * has_hi[0]
        az[pl.ds(0, nx, stride=ny), :] += faces[2 * ny : 2 * ny + nx, :] * has_lo[1]
        az[pl.ds(ny - 1, nx, stride=ny), :] += faces[2 * ny + nx : face_rows, :] * has_hi[1]
        corners = (
            (0, has_lo[0] * has_lo[1]),
            (ny - 1, has_lo[0] * has_hi[1]),
            (rows - ny, has_hi[0] * has_lo[1]),
            (rows - 1, has_hi[0] * has_hi[1]),
        )
        for n, (place, flag) in enumerate(corners):
            az[place : place + 1, :] += faces[face_rows + n : face_rows + n + 1, :] * flag
        drain(recvf.at[slot], sxy.at[slot])
        drain(recvz.at[slot], rzs.at[slot, 0])
        return az[...]

    mrows = crows + 1

    def plane_start(par):
        for n, o in enumerate(plane_peers):
            remote(
                msg.at[par, 0, pl.ds(0, mrows), :], arp.at[par, n], ssa.at[par, 0], rpa.at[par], o
            ).start()

    def plane_finish_line_start(par):
        drain(arp.at[par], rpa.at[par])
        msg[par, 1, 0:mrows] = msg[par, 0, 0:mrows] + jnp.sum(arp[par], axis=0)
        for n, o in enumerate(line_peers):
            remote(
                msg.at[par, 1, pl.ds(0, mrows), :], arz.at[par, n], ssa.at[par, 1], rza.at[par], o
            ).start()

    def line_finish(par):
        drain(arz.at[par], rza.at[par])
        total = msg[par, 1, 0:mrows] + jnp.sum(arz[par], axis=0)
        drain(arp.at[par], ssa.at[par, 0])
        drain(arz.at[par], ssa.at[par, 1])
        return total

    def grad(value):
        parts = parts_of(value)
        gxy = left_product(lxh[...], lxl[...], parts)
        return gxy, right_product(parts, rzh[...], rzl[...])

    def grad_transposed(wxy, wz):
        return left_product(lth[...], ltl[...], parts_of(wxy)) + right_product(
            parts_of(wz), rth[...], rtl[...]
        )

    def twice(value):
        return jnp.concatenate([value, value], axis=0)

    def total_of(value):
        return jnp.sum(jnp.sum(value, axis=0, keepdims=True), axis=1, keepdims=True)

    def spread(coarse):
        acc = jnp.zeros((16, nz), jnp.float32)
        for kz in range(3):
            product = xnb[kz, :, 0:LANES] * coarse[0:1, :]
            for j in range(1, crows):
                product = product + xnb[kz, :, j * LANES : (j + 1) * LANES] * coarse[j : j + 1, :]
            acc = acc + jnp.sum(product, axis=1, keepdims=True) * phi_z[kz]
        return exact(phi[...], acc, 0, 0)

    level = ls[...]
    gxy, gz = grad(level)
    advect = vel[0] * gxy[0:rows] + vel[1] * gxy[rows:] + vel[2] * gz
    b = mass[...]
    halo_start(b * advect, 0)
    halo_start(
        grad_transposed(jnp.concatenate([b * vel[0], b * vel[1]], axis=0), b * vel[2])
        + b * src[...],
        1,
    )
    level = level - TIME_STEP * halo_finish(0) * ibw[...]
    rhs = SOURCE_SCALE * halo_finish(1)
    rf[...] = rhs
    restricted = total_of(wt[...] * rhs)
    for j in range(crows):
        msg[1, 0, j : j + 1, :] = restricted * xrow[j : j + 1, :]
    plane_start(1)
    for sweep in range(RSWEEPS):
        gxy, gz = grad(level)
        gx, gy = gxy[0:rows], gxy[rows:]
        inv_norm = lax.rsqrt(1.0 + gx * gx + gy * gy + gz * gz)
        factor = mass[...] * (level * (1.0 - level) * inv_norm - INTERFACE_WIDTH)
        slot = (2 + sweep) % 3
        halo_start(grad_transposed(twice(factor) * gxy, factor * gz), slot)
        if sweep == 0:
            plane_finish_line_start(1)
        level = level + PSEUDO_STEP * halo_finish(slot) * ibw[...]
    lev_out[...] = level

    b = mass[...]
    sc = b / (GAS_DENSITY + (1.0 - GAS_DENSITY) * jnp.clip(level, 0.0, 1.0))
    scaled[...] = sc
    parts = parts_of(sc)
    halo_start(
        left_product(sqh[...], sql[...], parts) + right_product(parts, szh[...], szl[...]) + b, 1
    )
    coarse = line_finish(1)
    mv[0, 0:crows] = coarse[0:crows]
    drain(xin, xrs.at[0])
    drain(xin, xss.at[0])
    for n, o in enumerate(OFFSETS):
        for j in range(crows):
            xnb[1 - o[2], nine(o) : nine(o) + 1, j * LANES : (j + 1) * LANES] = xin[
                n * crows + j : n * crows + j + 1, :
            ]
    spread_now = spread(coarse)
    inverse = 1.0 / halo_finish(1)
    invd[...] = inverse
    zf[...] = rf[...] * inverse + spread_now

    def element_operator(value):
        gxy, gz = grad(value)
        sc = scaled[...]
        return grad_transposed(twice(sc) * gxy, sc * gz) + mass[...] * value

    lane1 = lax.broadcasted_iota(jnp.int32, (1, LANES), 1)

    def send_sums(par, z, q):
        inner = total_of(wt[...] * rf[...] * z)
        energy = total_of(q * z)
        cross = total_of(q * pf[...])
        msg[par, 0, crows : crows + 1, :] = jnp.where(
            lane1 == 0, inner, jnp.where(lane1 == 1, energy, jnp.where(lane1 == 2, cross, 0.0))
        )

    def steps_from(total, step):
        sums = total[crows : crows + 1, :]
        inner, energy, cross = sums[:, 0:1], sums[:, 1:2], sums[:, 2:3]
        old_inner, old_curve = mv[2, 0:1, 0:1], mv[2, 1:2, 0:1]
        ratio = jnp.where(step > 0, inner / old_inner, 0.0)
        curve = energy + 2.0 * ratio * cross + ratio * ratio * old_curve
        return inner, ratio, curve, inner / curve

    mv[2] = jnp.ones((8, LANES), jnp.float32)

    def iteration(step, carry):
        slot = lax.rem(step, 2)
        z = zf[...]
        q = element_operator(z)
        tested = exact(phi[...], q, 1, 0)
        columns = [jnp.sum(tested * phi_z[kz], axis=1, keepdims=True) for kz in range(3)]
        for j in range(crows):
            part = columns[0] * xnb[0, :, j * LANES : (j + 1) * LANES]
            for kz in (1, 2):
                part = part + columns[kz] * xnb[kz, :, j * LANES : (j + 1) * LANES]
            msg[slot, 0, j : j + 1, :] = jnp.sum(part, axis=0, keepdims=True)
        send_sums(slot, z, q)
        plane_start(slot)
        halo_start(q, slot)
        plane_finish_line_start(slot)
        az_now = halo_finish(slot)
        total = line_finish(slot)
        inner, ratio, curve, size = steps_from(total, step)
        p = z + ratio * pf[...]
        ap = az_now + ratio * apf[...]
        pf[...] = p
        apf[...] = ap
        p_out[...] += size * p
        r = rf[...] - size * ap
        rf[...] = r
        mv[1, 0:crows] = total[0:crows] + ratio * mv[1, 0:crows]
        coarse = mv[0, 0:crows] - size * mv[1, 0:crows]
        mv[0, 0:crows] = coarse
        mv[2, 0:1, :] = jnp.broadcast_to(inner, (1, LANES))
        mv[2, 1:2, :] = jnp.broadcast_to(curve, (1, LANES))
        zf[...] = r * invd[...] + spread(coarse)
        return carry

    lax.fori_loop(0, ITERS - 1, iteration, 0)

    par = (ITERS - 1) % 2
    z = zf[...]
    send_sums(par, z, element_operator(z))
    plane_start(par)
    plane_finish_line_start(par)
    _, ratio, _, size = steps_from(line_finish(par), ITERS - 1)
    p_out[...] += size * (z + ratio * pf[...])


def body(sizes, level_set, velocity, source, coarse_factor):
    nx, ny, nz = level_set.shape
    rows = nx * ny
    ncoarse = coarse_factor.shape[1]
    crows = ncoarse // LANES
    tables, mass = block_tables(nx, ny, nz)
    sx, sy, sz = sizes
    f32 = jnp.float32

    def vm(*shape):
        return pltpu.VMEM(shape, f32)

    dma = pltpu.SemaphoreType.DMA
    face_rows = 2 * ny + 2 * nx
    halves = rows // LANES
    scratch = [
        vm(3, rows, nz),
        vm(3, 2, nx, nz),
        vm(3, 9, 2 * halves, LANES),
        vm(3, face_rows + 4, nz),
        vm(3, 18 * halves, LANES),
        vm(rows, nz),
        vm(2, 2, 8, LANES),
        vm(2, sx * sy - 1, crows + 1, LANES),
        vm(2, sz - 1, crows + 1, LANES),
        vm(3, 16, ncoarse),
        vm(len(OFFSETS) * crows, LANES),
        vm(18, rows),
        vm(16, rows),
        vm(rows, nz),
        vm(rows, nz),
        vm(rows, nz),
        vm(rows, nz),
        vm(rows, nz),
        vm(rows, nz),
        vm(rows, nz),
        vm(rows, nz),
        vm(3, 8, LANES),
        vm(18, nz),
        dma((3,)),
        dma((3,)),
        dma((3, 2)),
        dma((2, 2)),
        dma((2,)),
        dma((2,)),
        dma((1,)),
        dma((1,)),
    ]
    flat = level_set.reshape(rows, nz)
    level, pressure = pl.pallas_call(
        functools.partial(kernel, (sizes, nx, ny, nz, ncoarse)),
        out_shape=(jax.ShapeDtypeStruct((rows, nz), f32),) * 2,
        in_specs=[pl.BlockSpec(memory_space=pltpu.VMEM)] * (5 + len(tables)),
        out_specs=(pl.BlockSpec(memory_space=pltpu.VMEM),) * 2,
        scratch_shapes=scratch,
        compiler_params=pltpu.CompilerParams(
            collective_id=0, has_side_effects=True, vmem_limit_bytes=48 * 1024 * 1024
        ),
        name="transport_and_pressure",
    )(
        flat,
        velocity.reshape(3, rows, nz),
        source.reshape(rows, nz),
        coarse_factor.reshape(crows, LANES),
        *[jnp.asarray(t) for t in tables],
        jnp.asarray(mass),
    )
    return level.reshape(nx, ny, nz), pressure.reshape(nx, ny, nz)


def solution(mesh):
    sizes = tuple(mesh.shape[a] for a in AXES)
    in_specs = (
        P("gx", "gy", "gz"),
        P(None, "gx", "gy", "gz"),
        P("gx", "gy", "gz"),
        P(("gx", "gy", "gz"), None),
    )
    out_specs = (P("gx", "gy", "gz"), P("gx", "gy", "gz"))
    return jax.shard_map(
        functools.partial(body, sizes),
        mesh=mesh,
        in_specs=in_specs,
        out_specs=out_specs,
        check_vma=False,
    )
```

```python
import functools

import jax
import jax.numpy as jnp
import numpy as np
from jax import lax
from jax.experimental import pallas as pl
from jax.experimental.pallas import tpu as pltpu
from jax.sharding import PartitionSpec as P

NP = 8
RSWEEPS = 2
ITERS = 6

GLL_POINTS = (
    -1.0,
    -0.8717401485096066,
    -0.5917001814331423,
    -0.2092992179024789,
    0.2092992179024789,
    0.5917001814331423,
    0.8717401485096066,
    1.0,
)
GLL_WEIGHTS = (
    0.03571428571428571,
    0.21070422714350603,
    0.3411226924835044,
    0.4124587946587038,
    0.4124587946587038,
    0.3411226924835044,
    0.21070422714350603,
    0.03571428571428571,
)
HIGHEST = lax.Precision.HIGHEST
TIME_STEP = 0.02
PSEUDO_STEP = 0.004
INTERFACE_WIDTH = 0.5
GAS_DENSITY = 0.1
SOURCE_SCALE = 20.0
MESH = pl.DeviceIdType.MESH
AXES = ("gx", "gy", "gz")
LANES = 128
OFFSETS = tuple(
    (i, j, k) for i in (-1, 0, 1) for j in (-1, 0, 1) for k in (-1, 0, 1) if (i, j, k) != (0, 0, 0)
)


def node_tables():
    points = np.array(GLL_POINTS)
    amount = points.shape[0]
    barycentric = np.ones(amount)
    for target in range(amount):
        for partner in range(amount):
            if partner != target:
                barycentric[target] = barycentric[target] / (points[target] - points[partner])
    derivative = np.zeros((amount, amount))
    for target in range(amount):
        for partner in range(amount):
            if partner != target:
                derivative[target, partner] = (
                    barycentric[partner] / barycentric[target] / (points[target] - points[partner])
                )
        derivative[target, target] = -np.sum(derivative[target])
    return derivative


def two_parts(matrix):
    matrix = matrix.astype(np.float32)
    high = matrix.astype(jnp.bfloat16)
    low = (matrix - high.astype(np.float32)).astype(jnp.bfloat16)
    return high, low


def block_tables(nx, ny, nz):
    d = node_tables()
    sq = (d * d).T

    def blocks(n, m):
        return np.kron(np.eye(n // NP), m)

    along_x = np.kron(blocks(nx, d), np.eye(ny))
    along_y = np.kron(np.eye(nx), blocks(ny, d))
    left = np.concatenate([along_x, along_y], axis=0)
    square = np.kron(blocks(nx, sq), np.eye(ny)) + np.kron(np.eye(nx), blocks(ny, sq))
    w = np.array(GLL_WEIGHTS, np.float32)
    rows = (np.tile(w, nx // NP)[:, None] * np.tile(w, ny // NP)[None, :]).reshape(-1, 1)
    mass = (rows * np.tile(w, nz // NP)[None, :]).astype(np.float32)
    tables = []
    for m in (left, left.T):
        tables.extend(two_parts(m))
    for m in (blocks(nz, d.T), blocks(nz, d)):
        high, low = two_parts(m)
        tables.extend((np.concatenate([high, low], axis=1), high))
    tables.append(np.stack(two_parts(square)))
    tables.append(np.concatenate(two_parts(blocks(nz, d * d)), axis=1))
    return tables + [mass]


def parts_of(value):
    high = value.astype(jnp.bfloat16)
    low = (value - high.astype(jnp.float32)).astype(jnp.bfloat16)
    return high, low


def mm(a, b):
    return jnp.dot(a, b, preferred_element_type=jnp.float32)


def left_product(high, low, value):
    a, b = parts_of(value)
    n = value.shape[1]
    wide = mm(high, jnp.concatenate([a, b], axis=1))
    return wide[:, :n] + (wide[:, n:] + mm(low, a))


def right_product(value, wide_table, high):
    a, b = parts_of(value)
    n = value.shape[1]
    wide = mm(a, wide_table)
    return wide[:, :n] + (wide[:, n:] + mm(b, high))


def exact(a, b, ca, cb):
    return lax.dot_general(
        a, b, (((ca,), (cb,)), ((), ())), precision=HIGHEST, preferred_element_type=jnp.float32
    )


def kernel(cfg, *refs):
    sizes, nx, ny, nz, ncoarse = cfg
    sx, sy, sz = sizes
    rows = nx * ny
    crows = ncoarse // LANES
    halves = rows // LANES
    given = refs[:15]
    lev_hbm, p_hbm = refs[15:17]
    held = refs[17:32]
    (ls, vel, src, xrow, lxh, lxl, lth, ltl, rzb, rzh, rtb, rth, sqb, szb, mass) = held
    (
        qs, ysend, zsend, recvf, recvz, az, msg, arp, arz, xnb, xin, zmask, phi, wt, ibw, scaled, invd,
        rf, zf, pf, apf, mv, ends, sxy, rxy, rzs, ssa, rpa, rza, xss, xrs,
        arps, arzs, phit, lsem, lev_out, p_out, osem,
    ) = refs[32:]

    loads = [pltpu.make_async_copy(a, b, lsem.at[n]) for n, (a, b) in enumerate(zip(given, held))]
    for n in (3, 14, 0, 4, 5, 8, 9, 1, 2, 6, 7, 10, 11, 12, 13):
        loads[n].start()

    me = [lax.axis_index(a) for a in AXES]

    def device(offset):
        return tuple(
            lax.rem(me[i] + (offset[i] % sizes[i]), sizes[i]) if offset[i] % sizes[i] else me[i]
            for i in range(3)
        )

    plane_peers = [(i, j, 0) for i in range(sx) for j in range(sy) if (i, j) != (0, 0)]
    line_peers = [(0, 0, k) for k in range(1, sz)]

    def distance(o):
        return sum(min(o[i] % sizes[i], -o[i] % sizes[i]) * (1 if i else 0.5) for i in range(3))

    plane_peers.sort(key=distance, reverse=True)
    line_peers.sort(key=distance, reverse=True)
    around = sorted(OFFSETS, key=lambda o: -sum(map(abs, o)))

    barrier = pltpu.get_barrier_semaphore()
    peers = sorted(
        {tuple(o[i] % sizes[i] for i in range(3)) for o in OFFSETS}
        | set(plane_peers)
        | set(line_peers)
    )
    for o in peers:
        pl.semaphore_signal(barrier, inc=1, device_id=device(o), device_id_type=MESH)

    has_lo = [jnp.where(me[i] > 0, 1.0, 0.0).astype(jnp.float32) for i in range(3)]
    has_hi = [jnp.where(me[i] < sizes[i] - 1, 1.0, 0.0).astype(jnp.float32) for i in range(3)]

    row = lax.broadcasted_iota(jnp.int32, (rows, 1), 0)
    lane = lax.broadcasted_iota(jnp.int32, (1, nz), 1)
    row_x, row_y = lax.shift_right_logical(row, ny.bit_length() - 1), lax.bitwise_and(row, ny - 1)

    def inverse_copies(index, extent, dim):
        inside = lax.bitwise_and(index, NP - 1)
        low = (inside == 0) & (index > 0)
        high = (inside == NP - 1) & (index < extent - 1)
        value = jnp.where(low | high, 0.5, 1.0).astype(jnp.float32)
        value = value - jnp.where(index == 0, 0.5, 0.0) * has_lo[dim]
        return value - jnp.where(index == extent - 1, 0.5, 0.0) * has_hi[dim]

    weight = inverse_copies(row_x, nx, 0) * inverse_copies(row_y, ny, 1) * inverse_copies(lane, nz, 2)
    wt[...] = weight
    loads[14].wait()
    ibw[...] = weight / mass[...]

    def spread_shape(index, extent, dim, which):
        at_low = jnp.where(index == 0, 0.5, 0.0) * has_lo[dim]
        at_high = jnp.where(index == extent - 1, 0.5, 0.0) * has_hi[dim]
        own = 1.0 - at_low - at_high
        return jnp.where(which == 0, at_low, jnp.where(which == 1, own, at_high))

    flat = lax.broadcasted_iota(jnp.int32, (1, rows), 1)
    flat_x = lax.shift_right_logical(flat, ny.bit_length() - 1)
    flat_y = lax.bitwise_and(flat, ny - 1)

    def split_nine(count):
        k = lax.broadcasted_iota(jnp.int32, (count, 1), 0)
        first = jnp.where(k >= 3, 1, 0) + jnp.where(k >= 6, 1, 0)
        return k, first, k - 3 * first

    k9, kx, ky = split_nine(16)
    both = spread_shape(flat_x, nx, 0, kx) * spread_shape(flat_y, ny, 1, ky)
    phi[...] = jnp.where(k9 < 9, both, 0.0)
    k48 = lax.broadcasted_iota(jnp.int32, (1, 48), 1)
    k48 = lax.bitwise_and(k48, 15)
    first = jnp.where(k48 >= 3, 1, 0) + jnp.where(k48 >= 6, 1, 0)
    both = spread_shape(row_x, nx, 0, first) * spread_shape(row_y, ny, 1, k48 - 3 * first)
    phit[...] = jnp.where(k48 < 9, both, 0.0).astype(jnp.bfloat16)
    phi_z = [spread_shape(lane, nz, 2, jnp.full((1, nz), kz, jnp.int32)) for kz in range(3)]

    k18 = lax.broadcasted_iota(jnp.int32, (18, 1), 0)
    upper = jnp.where(k18 >= 9, 1, 0)
    k_in = k18 - 9 * upper
    zx = jnp.where(k_in >= 3, 1, 0) + jnp.where(k_in >= 6, 1, 0)
    zy = k_in - 3 * zx

    def region(index, extent, dim, which):
        at_low = jnp.where(index == 0, 1.0, 0.0) * has_lo[dim]
        at_high = jnp.where(index == extent - 1, 1.0, 0.0) * has_hi[dim]
        return jnp.where(which == 0, at_low, jnp.where(which == 1, 1.0, at_high))

    side = jnp.where(upper == 0, has_lo[2], has_hi[2])
    zmask[...] = region(flat_x, nx, 0, zx) * region(flat_y, ny, 1, zy) * side
    wide_lane = lax.broadcasted_iota(jnp.int32, (18, nz), 1)
    target = jnp.where(k18 < 9, 0, nz - 1)
    ends[...] = jnp.where(wide_lane == target, 1.0, 0.0)
    xnb[...] = jnp.zeros_like(xnb)
    loads[3].wait()
    for j in range(crows):
        xnb[1, 4:5, j * LANES : (j + 1) * LANES] = xrow[j : j + 1, :]
    for par in range(2):
        msg[par] = jnp.zeros_like(msg[par])
    pf[...] = jnp.zeros_like(pf)
    apf[...] = jnp.zeros_like(apf)
    mv[...] = jnp.zeros_like(mv)
    p_out[...] = jnp.zeros_like(p_out)

    def remote(source, dest, send, recv, offset):
        return pltpu.make_async_remote_copy(
            src_ref=source,
            dst_ref=dest,
            send_sem=send,
            recv_sem=recv,
            device_id=device(offset),
            device_id_type=MESH,
        )

    def drain(ref, sem):
        pltpu.make_async_copy(ref, ref, sem).wait()

    def nine(o):
        return (1 - o[0]) * 3 + (1 - o[1])

    face_rows = 2 * ny + 2 * nx

    def halo_pack(value, slot):
        inside = lax.bitwise_and(lane, NP - 1)
        up = (inside == NP - 1) & (lane < nz - 1)
        down = (inside == 0) & (lane > 0)
        q = (
            value
            + jnp.where(up, pltpu.roll(value, nz - 1, 1), 0.0)
            + jnp.where(down, pltpu.roll(value, 1, 1), 0.0)
        )
        field = qs.at[slot]
        field[...] = q
        for e in range(NP, ny, NP):
            total = field[pl.ds(e - 1, nx, stride=ny), :] + field[pl.ds(e, nx, stride=ny), :]
            field[pl.ds(e - 1, nx, stride=ny), :] = total
            field[pl.ds(e, nx, stride=ny), :] = total
        for e in range(NP, nx, NP):
            total = field[(e - 1) * ny : e * ny, :] + field[e * ny : (e + 1) * ny, :]
            field[(e - 1) * ny : e * ny, :] = total
            field[e * ny : (e + 1) * ny, :] = total
        ysend[slot, 0] = field[pl.ds(0, nx, stride=ny), :]
        ysend[slot, 1] = field[pl.ds(ny - 1, nx, stride=ny), :]
        across = jnp.transpose(field[...])
        face = jnp.concatenate([across[0:1], across[nz - 1 : nz]], axis=0)
        for dx in (-1, 0, 1):
            for dy in (-1, 0, 1):
                shift = (-ny * dx + (ny - 1) * dy) % rows
                moved = pltpu.roll(face, shift, 1) if shift else face
                place = (dx + 1) * 3 + dy + 1
                for h in range(halves):
                    part = moved[0:2, h * LANES : (h + 1) * LANES]
                    zsend[slot, place, h : h + 1, :] = part[0:1]
                    zsend[slot, place, halves + h : halves + h + 1, :] = part[1:2]

    def halo_send(slot):
        send, recv = sxy.at[slot], rxy.at[slot]
        for o in around:
            if o[2] != 0:
                k, hi = nine(o), 1 if o[2] > 0 else 0
                remote(
                    zsend.at[slot, k, pl.ds(hi * halves, halves), :],
                    recvz.at[slot, pl.ds((k + (0 if hi else 9)) * halves, halves), :],
                    rzs.at[slot, 0],
                    rzs.at[slot, 1],
                    o,
                ).start()
        for o in around:
            if o[2] == 0:
                x_row = 0 if o[0] < 0 else (nx - 1) * ny
                y_row = 0 if o[1] < 0 else ny - 1
                if o[1] == 0:
                    source = qs.at[slot, pl.ds(x_row, ny), :]
                    place, count = (0 if o[0] > 0 else ny), ny
                elif o[0] == 0:
                    source = ysend.at[slot, 0 if o[1] < 0 else 1]
                    place, count = 2 * ny + (0 if o[1] > 0 else nx), nx
                else:
                    source = qs.at[slot, pl.ds(x_row + y_row, 1), :]
                    place = face_rows + (0 if o[0] > 0 else 2) + (0 if o[1] > 0 else 1)
                    count = 1
                remote(source, recvf.at[slot, pl.ds(place, count), :], send, recv, o).start()

    def halo_start(value, slot):
        halo_pack(value, slot)
        halo_send(slot)

    def halo_finish(slot):
        drain(recvf.at[slot], rxy.at[slot])
        drain(recvz.at[slot], rzs.at[slot, 1])
        for h in range(halves):
            piece = slice(h * LANES, (h + 1) * LANES)
            arrived = recvz[slot, pl.ds(h, 18, stride=halves), :] * zmask[:, piece]
            az[piece, :] = qs[slot, piece, :] + exact(arrived, ends[...], 0, 0)
        faces = recvf.at[slot]
        az[0:ny, :] += faces[0:ny, :] * has_lo[0]
        az[rows - ny : rows, :] += faces[ny : 2 * ny, :] * has_hi[0]
        az[pl.ds(0, nx, stride=ny), :] += faces[2 * ny : 2 * ny + nx, :] * has_lo[1]
        az[pl.ds(ny - 1, nx, stride=ny), :] += faces[2 * ny + nx : face_rows, :] * has_hi[1]
        corners = (
            (0, has_lo[0] * has_lo[1]),
            (ny - 1, has_lo[0] * has_hi[1]),
            (rows - ny, has_hi[0] * has_lo[1]),
            (rows - 1, has_hi[0] * has_hi[1]),
        )
        for n, (place, flag) in enumerate(corners):
            az[place : place + 1, :] += faces[face_rows + n : face_rows + n + 1, :] * flag
        drain(recvf.at[slot], sxy.at[slot])
        drain(recvz.at[slot], rzs.at[slot, 0])
        return az[...]

    mrows = crows + 1

    def plane_start(par):
        for n, o in enumerate(plane_peers):
            remote(
                msg.at[par, 0, pl.ds(0, mrows), :], arp.at[par, n], ssa.at[par, 0], rpa.at[par], o
            ).start()

    def sum_of_row():
        own = pl.ds(crows, 1)
        for n, o in enumerate(plane_peers):
            place = arps.at[pl.ds(n, 1), :]
            remote(msg.at[1, 0, own, :], place, ssa.at[2, 0], rpa.at[2], o).start()
        drain(arps, rpa.at[2])
        here = msg[1, 0, crows : crows + 1] + jnp.sum(arps[...], axis=0, keepdims=True)
        msg[1, 1, crows : crows + 1] = here
        for n, o in enumerate(line_peers):
            place = arzs.at[pl.ds(n, 1), :]
            remote(msg.at[1, 1, own, :], place, ssa.at[2, 1], rza.at[2], o).start()
        drain(arzs, rza.at[2])
        drain(arps, ssa.at[2, 0])
        drain(arzs, ssa.at[2, 1])
        return here + jnp.sum(arzs[...], axis=0, keepdims=True)

    def plane_finish_line_start(par):
        drain(arp.at[par], rpa.at[par])
        msg[par, 1, 0:mrows] = msg[par, 0, 0:mrows] + jnp.sum(arp[par], axis=0)
        for n, o in enumerate(line_peers):
            remote(
                msg.at[par, 1, pl.ds(0, mrows), :], arz.at[par, n], ssa.at[par, 1], rza.at[par], o
            ).start()

    def line_finish(par):
        drain(arz.at[par], rza.at[par])
        total = msg[par, 1, 0:mrows] + jnp.sum(arz[par], axis=0)
        drain(arp.at[par], ssa.at[par, 0])
        drain(arz.at[par], ssa.at[par, 1])
        return total

    def grad(value):
        gxy = left_product(lxh[...], lxl[...], value)
        return gxy, right_product(value, rzb[...], rzh[...])

    def grad_transposed(wxy, wz):
        return left_product(lth[...], ltl[...], wxy) + right_product(wz, rtb[...], rth[...])

    def twice(value):
        return jnp.concatenate([value, value], axis=0)

    def total_of(value):
        return jnp.sum(jnp.sum(value, axis=0, keepdims=True), axis=1, keepdims=True)

    def spread(coarse):
        acc = jnp.zeros((16, nz), jnp.float32)
        for kz in range(3):
            product = xnb[kz, :, 0:LANES] * coarse[0:1, :]
            for j in range(1, crows):
                product = product + xnb[kz, :, j * LANES : (j + 1) * LANES] * coarse[j : j + 1, :]
            acc = acc + jnp.sum(product, axis=1, keepdims=True) * phi_z[kz]
        high, low = parts_of(acc)
        rest = (acc - high.astype(jnp.float32) - low.astype(jnp.float32)).astype(jnp.bfloat16)
        return mm(phit[...], jnp.concatenate([high, low, rest], axis=0))

    for n in (0, 4, 5, 8, 9, 1):
        loads[n].wait()
    level = ls[...]
    gxy, gz = grad(level)
    advect = vel[0] * gxy[0:rows] + vel[1] * gxy[rows:] + vel[2] * gz
    b = mass[...]
    halo_pack(b * advect, 0)
    for n in (2, 6, 7, 10, 11):
        loads[n].wait()
    halo_pack(
        grad_transposed(jnp.concatenate([b * vel[0], b * vel[1]], axis=0), b * vel[2])
        + b * src[...],
        1,
    )
    pl.semaphore_wait(barrier, len(peers))
    halo_send(0)
    halo_send(1)
    for o in OFFSETS:
        place = pl.ds(OFFSETS.index(o) * crows, crows)
        remote(xrow, xin.at[place, :], xss.at[0], xrs.at[0], o).start()
    level = level - TIME_STEP * halo_finish(0) * ibw[...]
    for sweep in range(RSWEEPS):
        gxy, gz = grad(level)
        gx, gy = gxy[0:rows], gxy[rows:]
        inv_norm = lax.rsqrt(1.0 + gx * gx + gy * gy + gz * gz)
        factor = mass[...] * (level * (1.0 - level) * inv_norm - INTERFACE_WIDTH)
        slot = (2 + sweep) % 3
        halo_start(grad_transposed(twice(factor) * gxy, factor * gz), slot)
        if sweep == 0:
            rhs = SOURCE_SCALE * halo_finish(1)
            rf[...] = rhs
            restricted = total_of(wt[...] * rhs)
            for j in range(crows):
                msg[1, 0, j : j + 1, :] = restricted * xrow[j : j + 1, :]
            plane_start(1)
        else:
            plane_finish_line_start(1)
        level = level + PSEUDO_STEP * halo_finish(slot) * ibw[...]
    lev_out[...] = level
    level_copy = pltpu.make_async_copy(lev_out, lev_hbm, osem.at[0])
    level_copy.start()

    b = mass[...]
    sc = b / (GAS_DENSITY + (1.0 - GAS_DENSITY) * jnp.clip(level, 0.0, 1.0))
    scaled[...] = sc
    for n in (12, 13):
        loads[n].wait()
    halo_start(
        left_product(sqb[0], sqb[1], sc) + right_product(sc, szb[...], szb[:, 0:nz]) + b, 1
    )
    coarse = line_finish(1)
    mv[0, 0:crows] = coarse[0:crows]
    drain(xin, xrs.at[0])
    drain(xin, xss.at[0])
    for n, o in enumerate(OFFSETS):
        for j in range(crows):
            xnb[1 - o[2], nine(o) : nine(o) + 1, j * LANES : (j + 1) * LANES] = xin[
                n * crows + j : n * crows + j + 1, :
            ]
    spread_now = spread(coarse)
    inverse = 1.0 / halo_finish(1)
    invd[...] = inverse
    zf[...] = rf[...] * inverse + spread_now

    def element_operator(value):
        gxy, gz = grad(value)
        sc = scaled[...]
        return grad_transposed(twice(sc) * gxy, sc * gz) + mass[...] * value

    lane1 = lax.broadcasted_iota(jnp.int32, (1, LANES), 1)

    def send_sums(par, z, q):
        inner = total_of(wt[...] * rf[...] * z)
        energy = total_of(q * z)
        cross = total_of(q * pf[...])
        msg[par, 0, crows : crows + 1, :] = jnp.where(
            lane1 == 0, inner, jnp.where(lane1 == 1, energy, jnp.where(lane1 == 2, cross, 0.0))
        )

    def steps_from(sums, step):
        inner, energy, cross = sums[:, 0:1], sums[:, 1:2], sums[:, 2:3]
        old_inner, old_curve = mv[2, 0:1, 0:1], mv[2, 1:2, 0:1]
        ratio = jnp.where(step > 0, inner / old_inner, 0.0)
        curve = energy + 2.0 * ratio * cross + ratio * ratio * old_curve
        return inner, ratio, curve, inner / curve

    mv[2] = jnp.ones((8, LANES), jnp.float32)

    def iteration(step, carry):
        slot = lax.rem(step, 2)
        z = zf[...]
        q = element_operator(z)
        high, low = parts_of(q)
        wide = mm(phi[...].astype(jnp.bfloat16), jnp.concatenate([high, low], axis=1))
        tested = wide[:, :nz] + wide[:, nz:]
        columns = [jnp.sum(tested * phi_z[kz], axis=1, keepdims=True) for kz in range(3)]
        for j in range(crows):
            part = columns[0] * xnb[0, :, j * LANES : (j + 1) * LANES]
            for kz in (1, 2):
                part = part + columns[kz] * xnb[kz, :, j * LANES : (j + 1) * LANES]
            msg[slot, 0, j : j + 1, :] = jnp.sum(part, axis=0, keepdims=True)
        send_sums(slot, z, q)
        plane_start(slot)
        halo_start(q, slot)
        plane_finish_line_start(slot)
        az_now = halo_finish(slot)
        total = line_finish(slot)
        inner, ratio, curve, size = steps_from(total[crows : crows + 1, :], step)
        p = z + ratio * pf[...]
        ap = az_now + ratio * apf[...]
        pf[...] = p
        apf[...] = ap
        p_out[...] += size * p
        r = rf[...] - size * ap
        rf[...] = r
        mv[1, 0:crows] = total[0:crows] + ratio * mv[1, 0:crows]
        coarse = mv[0, 0:crows] - size * mv[1, 0:crows]
        mv[0, 0:crows] = coarse
        mv[2, 0:1, :] = jnp.broadcast_to(inner, (1, LANES))
        mv[2, 1:2, :] = jnp.broadcast_to(curve, (1, LANES))
        zf[...] = r * invd[...] + spread(coarse)
        return carry

    lax.fori_loop(0, ITERS - 1, iteration, 0)

    z = zf[...]
    send_sums(1, z, element_operator(z))
    _, ratio, _, size = steps_from(sum_of_row(), ITERS - 1)
    p_out[...] += size * (z + ratio * pf[...])
    pressure_copy = pltpu.make_async_copy(p_out, p_hbm, osem.at[1])
    pressure_copy.start()
    level_copy.wait()
    pressure_copy.wait()


def body(sizes, level_set, velocity, source, coarse_factor):
    nx, ny, nz = level_set.shape
    rows = nx * ny
    ncoarse = coarse_factor.shape[1]
    crows = ncoarse // LANES
    tables = block_tables(nx, ny, nz)
    sx, sy, sz = sizes
    f32 = jnp.float32

    def vm(*shape):
        return pltpu.VMEM(shape, f32)

    dma = pltpu.SemaphoreType.DMA
    face_rows = 2 * ny + 2 * nx
    halves = rows // LANES
    operands = [
        level_set.reshape(rows, nz),
        velocity.reshape(3, rows, nz),
        source.reshape(rows, nz),
        coarse_factor.reshape(crows, LANES),
        *[jnp.asarray(t) for t in tables],
    ]
    scratch = [pltpu.VMEM(a.shape, a.dtype) for a in operands] + [
        vm(3, rows, nz),
        vm(3, 2, nx, nz),
        vm(3, 9, 2 * halves, LANES),
        vm(3, face_rows + 4, nz),
        vm(3, 18 * halves, LANES),
        vm(rows, nz),
        vm(2, 2, 8, LANES),
        vm(2, sx * sy - 1, crows + 1, LANES),
        vm(2, sz - 1, crows + 1, LANES),
        vm(3, 16, ncoarse),
        vm(len(OFFSETS) * crows, LANES),
        vm(18, rows),
        vm(16, rows),
        vm(rows, nz),
        vm(rows, nz),
        vm(rows, nz),
        vm(rows, nz),
        vm(rows, nz),
        vm(rows, nz),
        vm(rows, nz),
        vm(rows, nz),
        vm(3, 8, LANES),
        vm(18, nz),
        dma((3,)),
        dma((3,)),
        dma((3, 2)),
        dma((3, 2)),
        dma((3,)),
        dma((3,)),
        dma((1,)),
        dma((1,)),
        vm(sx * sy - 1, LANES),
        vm(sz - 1, LANES),
        pltpu.VMEM((rows, 48), jnp.bfloat16),
        dma((len(operands),)),
        vm(rows, nz),
        vm(rows, nz),
        dma((2,)),
    ]
    level, pressure = pl.pallas_call(
        functools.partial(kernel, (sizes, nx, ny, nz, ncoarse)),
        out_shape=(jax.ShapeDtypeStruct((rows, nz), f32),) * 2,
        in_specs=[pl.BlockSpec(memory_space=pltpu.HBM)] * len(operands),
        out_specs=(pl.BlockSpec(memory_space=pltpu.HBM),) * 2,
        scratch_shapes=scratch,
        compiler_params=pltpu.CompilerParams(
            collective_id=0, has_side_effects=True, vmem_limit_bytes=63 * 1024 * 1024
        ),
        name="transport_and_pressure",
    )(*operands)
    return level.reshape(nx, ny, nz), pressure.reshape(nx, ny, nz)


def solution(mesh):
    sizes = tuple(mesh.shape[a] for a in AXES)
    in_specs = (
        P("gx", "gy", "gz"),
        P(None, "gx", "gy", "gz"),
        P("gx", "gy", "gz"),
        P(("gx", "gy", "gz"), None),
    )
    out_specs = (P("gx", "gy", "gz"), P("gx", "gy", "gz"))
    return jax.shard_map(
        functools.partial(body, sizes),
        mesh=mesh,
        in_specs=in_specs,
        out_specs=out_specs,
        check_vma=False,
    )
```

```python
import functools

import jax
import jax.numpy as jnp
import numpy as np
from jax import lax
from jax.experimental import pallas as pl
from jax.experimental.pallas import tpu as pltpu
from jax.sharding import PartitionSpec as P

NP = 8
RSWEEPS = 2
ITERS = 6

GLL_POINTS = (
    -1.0,
    -0.8717401485096066,
    -0.5917001814331423,
    -0.2092992179024789,
    0.2092992179024789,
    0.5917001814331423,
    0.8717401485096066,
    1.0,
)
GLL_WEIGHTS = (
    0.03571428571428571,
    0.21070422714350603,
    0.3411226924835044,
    0.4124587946587038,
    0.4124587946587038,
    0.3411226924835044,
    0.21070422714350603,
    0.03571428571428571,
)
HIGHEST = lax.Precision.HIGHEST
TIME_STEP = 0.02
PSEUDO_STEP = 0.004
INTERFACE_WIDTH = 0.5
GAS_DENSITY = 0.1
SOURCE_SCALE = 20.0
MESH = pl.DeviceIdType.MESH
AXES = ("gx", "gy", "gz")
LANES = 128
OFFSETS = tuple(
    (i, j, k) for i in (-1, 0, 1) for j in (-1, 0, 1) for k in (-1, 0, 1) if (i, j, k) != (0, 0, 0)
)


def node_tables():
    points = np.array(GLL_POINTS)
    amount = points.shape[0]
    barycentric = np.ones(amount)
    for target in range(amount):
        for partner in range(amount):
            if partner != target:
                barycentric[target] = barycentric[target] / (points[target] - points[partner])
    derivative = np.zeros((amount, amount))
    for target in range(amount):
        for partner in range(amount):
            if partner != target:
                derivative[target, partner] = (
                    barycentric[partner] / barycentric[target] / (points[target] - points[partner])
                )
        derivative[target, target] = -np.sum(derivative[target])
    return derivative


def two_parts(matrix):
    matrix = matrix.astype(np.float32)
    high = matrix.astype(jnp.bfloat16)
    low = (matrix - high.astype(np.float32)).astype(jnp.bfloat16)
    return high, low


def block_tables(nx, ny, nz):
    d = node_tables()
    sq = (d * d).T

    def blocks(n, m):
        return np.kron(np.eye(n // NP), m)

    along_x = np.kron(blocks(nx, d), np.eye(ny))
    along_y = np.kron(np.eye(nx), blocks(ny, d))
    left = np.concatenate([along_x, along_y], axis=0)
    square = np.kron(blocks(nx, sq), np.eye(ny)) + np.kron(np.eye(nx), blocks(ny, sq))
    w = np.array(GLL_WEIGHTS, np.float32)
    rows = (np.tile(w, nx // NP)[:, None] * np.tile(w, ny // NP)[None, :]).reshape(-1, 1)
    mass = (rows * np.tile(w, nz // NP)[None, :]).astype(np.float32)
    tables = []
    for m in (left, left.T):
        tables.extend(two_parts(m))
    for m in (blocks(nz, d.T), blocks(nz, d)):
        high, low = two_parts(m)
        tables.extend((np.concatenate([high, low], axis=1), high))
    tables.append(np.stack(two_parts(square)))
    tables.append(np.concatenate(two_parts(blocks(nz, d * d)), axis=1))
    return tables + [mass]


def parts_of(value):
    high = value.astype(jnp.bfloat16)
    low = (value - high.astype(jnp.float32)).astype(jnp.bfloat16)
    return high, low


def mm(a, b):
    return jnp.dot(a, b, preferred_element_type=jnp.float32)


def left_product(high, low, value):
    a, b = parts_of(value)
    n = value.shape[1]
    wide = mm(high, jnp.concatenate([a, b], axis=1))
    return wide[:, :n] + (wide[:, n:] + mm(low, a))


def right_product(value, wide_table, high):
    a, b = parts_of(value)
    n = value.shape[1]
    wide = mm(a, wide_table)
    return wide[:, :n] + (wide[:, n:] + mm(b, high))


def kernel(cfg, *refs):
    sizes, nx, ny, nz, ncoarse = cfg
    sx, sy, sz = sizes
    rows = nx * ny
    crows = ncoarse // LANES
    halves = rows // LANES
    given = refs[:15]
    lev_hbm, p_hbm = refs[15:17]
    held = refs[17:32]
    (ls, vel, src, xrow, lxh, lxl, lth, ltl, rzb, rzh, rtb, rth, sqb, szb, mass) = held
    (
        qs, ysend, zsend, recvf, recvz, az, msg, arp, arz, xnb, xin, zmask, phi, wt, ibw, scaled, invd,
        rf, zf, pf, apf, mv, sxy, rxy, rzs, ssa, rpa, rza, xss, xrs,
        arps, arzs, phit, lsem, lev_out, p_out, osem,
    ) = refs[32:]

    loads = [pltpu.make_async_copy(a, b, lsem.at[n]) for n, (a, b) in enumerate(zip(given, held))]

    me = [lax.axis_index(a) for a in AXES]

    def device(offset):
        return tuple(
            lax.rem(me[i] + (offset[i] % sizes[i]), sizes[i]) if offset[i] % sizes[i] else me[i]
            for i in range(3)
        )

    plane_peers = [(i, j, 0) for i in range(sx) for j in range(sy) if (i, j) != (0, 0)]
    line_peers = [(0, 0, k) for k in range(1, sz)]

    def distance(o):
        return sum(min(o[i] % sizes[i], -o[i] % sizes[i]) * (1 if i else 0.5) for i in range(3))

    plane_peers.sort(key=distance, reverse=True)
    line_peers.sort(key=distance, reverse=True)
    around = sorted(OFFSETS, key=lambda o: -sum(map(abs, o)))

    barrier = pltpu.get_barrier_semaphore()
    peers = sorted(
        {tuple(o[i] % sizes[i] for i in range(3)) for o in OFFSETS}
        | set(plane_peers)
        | set(line_peers)
    )
    peers.sort(key=distance, reverse=True)
    for o in peers:
        pl.semaphore_signal(barrier, inc=1, device_id=device(o), device_id_type=MESH)
    for n in (3, 14, 0, 4, 5, 8, 9, 1, 2, 6, 7, 10, 11, 12, 13):
        loads[n].start()

    has_lo = [jnp.where(me[i] > 0, 1.0, 0.0).astype(jnp.float32) for i in range(3)]
    has_hi = [jnp.where(me[i] < sizes[i] - 1, 1.0, 0.0).astype(jnp.float32) for i in range(3)]

    row = lax.broadcasted_iota(jnp.int32, (rows, 1), 0)
    lane = lax.broadcasted_iota(jnp.int32, (1, nz), 1)
    row_x, row_y = lax.shift_right_logical(row, ny.bit_length() - 1), lax.bitwise_and(row, ny - 1)

    def inverse_copies(index, extent, dim):
        inside = lax.bitwise_and(index, NP - 1)
        low = (inside == 0) & (index > 0)
        high = (inside == NP - 1) & (index < extent - 1)
        value = jnp.where(low | high, 0.5, 1.0).astype(jnp.float32)
        value = value - jnp.where(index == 0, 0.5, 0.0) * has_lo[dim]
        return value - jnp.where(index == extent - 1, 0.5, 0.0) * has_hi[dim]

    weight = inverse_copies(row_x, nx, 0) * inverse_copies(row_y, ny, 1) * inverse_copies(lane, nz, 2)
    wt[...] = weight
    loads[14].wait()
    ibw[...] = weight / mass[...]

    def spread_shape(index, extent, dim, which):
        at_low = jnp.where(index == 0, 0.5, 0.0) * has_lo[dim]
        at_high = jnp.where(index == extent - 1, 0.5, 0.0) * has_hi[dim]
        own = 1.0 - at_low - at_high
        return jnp.where(which == 0, at_low, jnp.where(which == 1, own, at_high))

    flat = lax.broadcasted_iota(jnp.int32, (1, rows), 1)
    flat_x = lax.shift_right_logical(flat, ny.bit_length() - 1)
    flat_y = lax.bitwise_and(flat, ny - 1)

    def split_nine(count):
        k = lax.broadcasted_iota(jnp.int32, (count, 1), 0)
        first = jnp.where(k >= 3, 1, 0) + jnp.where(k >= 6, 1, 0)
        return k, first, k - 3 * first

    k9, kx, ky = split_nine(16)
    both = spread_shape(flat_x, nx, 0, kx) * spread_shape(flat_y, ny, 1, ky)
    phi[...] = jnp.where(k9 < 9, both, 0.0)
    k48 = lax.broadcasted_iota(jnp.int32, (1, 48), 1)
    k48 = lax.bitwise_and(k48, 15)
    first = jnp.where(k48 >= 3, 1, 0) + jnp.where(k48 >= 6, 1, 0)
    both = spread_shape(row_x, nx, 0, first) * spread_shape(row_y, ny, 1, k48 - 3 * first)
    phit[...] = jnp.where(k48 < 9, both, 0.0).astype(jnp.bfloat16)
    phi_z = [spread_shape(lane, nz, 2, jnp.full((1, nz), kz, jnp.int32)) for kz in range(3)]

    k18 = lax.broadcasted_iota(jnp.int32, (18, 1), 0)
    upper = jnp.where(k18 >= 9, 1, 0)
    k_in = k18 - 9 * upper
    zx = jnp.where(k_in >= 3, 1, 0) + jnp.where(k_in >= 6, 1, 0)
    zy = k_in - 3 * zx

    def region(index, extent, dim, which):
        at_low = jnp.where(index == 0, 1.0, 0.0) * has_lo[dim]
        at_high = jnp.where(index == extent - 1, 1.0, 0.0) * has_hi[dim]
        return jnp.where(which == 0, at_low, jnp.where(which == 1, 1.0, at_high))

    side = jnp.where(upper == 0, has_lo[2], has_hi[2])
    zmask[...] = region(flat_x, nx, 0, zx) * region(flat_y, ny, 1, zy) * side
    xnb[...] = jnp.zeros_like(xnb)
    loads[3].wait()
    for j in range(crows):
        xnb[1, 4:5, j * LANES : (j + 1) * LANES] = xrow[j : j + 1, :]
    for par in range(2):
        msg[par] = jnp.zeros_like(msg[par])
    pf[...] = jnp.zeros_like(pf)
    apf[...] = jnp.zeros_like(apf)
    mv[...] = jnp.zeros_like(mv)
    p_out[...] = jnp.zeros_like(p_out)

    def remote(source, dest, send, recv, offset):
        return pltpu.make_async_remote_copy(
            src_ref=source,
            dst_ref=dest,
            send_sem=send,
            recv_sem=recv,
            device_id=device(offset),
            device_id_type=MESH,
        )

    def drain(ref, sem):
        pltpu.make_async_copy(ref, ref, sem).wait()

    def nine(o):
        return (1 - o[0]) * 3 + (1 - o[1])

    face_rows = 2 * ny + 2 * nx

    def halo_pack(value, slot):
        inside = lax.bitwise_and(lane, NP - 1)
        up = (inside == NP - 1) & (lane < nz - 1)
        down = (inside == 0) & (lane > 0)
        q = (
            value
            + jnp.where(up, pltpu.roll(value, nz - 1, 1), 0.0)
            + jnp.where(down, pltpu.roll(value, 1, 1), 0.0)
        )
        field = qs.at[slot]
        field[...] = q
        for e in range(NP, ny, NP):
            total = field[pl.ds(e - 1, nx, stride=ny), :] + field[pl.ds(e, nx, stride=ny), :]
            field[pl.ds(e - 1, nx, stride=ny), :] = total
            field[pl.ds(e, nx, stride=ny), :] = total
        for e in range(NP, nx, NP):
            total = field[(e - 1) * ny : e * ny, :] + field[e * ny : (e + 1) * ny, :]
            field[(e - 1) * ny : e * ny, :] = total
            field[e * ny : (e + 1) * ny, :] = total
        ysend[slot, 0] = field[pl.ds(0, nx, stride=ny), :]
        ysend[slot, 1] = field[pl.ds(ny - 1, nx, stride=ny), :]
        across = jnp.transpose(field[...])
        face = jnp.concatenate([across[0:1], across[nz - 1 : nz]], axis=0)
        for dx in (-1, 0, 1):
            for dy in (-1, 0, 1):
                shift = (-ny * dx + (ny - 1) * dy) % rows
                moved = pltpu.roll(face, shift, 1) if shift else face
                place = (dx + 1) * 3 + dy + 1
                for h in range(halves):
                    part = moved[0:2, h * LANES : (h + 1) * LANES]
                    zsend[slot, place, h : h + 1, :] = part[0:1]
                    zsend[slot, place, halves + h : halves + h + 1, :] = part[1:2]

    def halo_send(slot):
        send, recv = sxy.at[slot], rxy.at[slot]
        for o in around:
            if o[2] != 0:
                k, hi = nine(o), 1 if o[2] > 0 else 0
                remote(
                    zsend.at[slot, k, pl.ds(hi * halves, halves), :],
                    recvz.at[slot, pl.ds((k + (0 if hi else 9)) * halves, halves), :],
                    rzs.at[slot, 0],
                    rzs.at[slot, 1],
                    o,
                ).start()
        for o in around:
            if o[2] == 0:
                x_row = 0 if o[0] < 0 else (nx - 1) * ny
                y_row = 0 if o[1] < 0 else ny - 1
                if o[1] == 0:
                    source = qs.at[slot, pl.ds(x_row, ny), :]
                    place, count = (0 if o[0] > 0 else ny), ny
                elif o[0] == 0:
                    source = ysend.at[slot, 0 if o[1] < 0 else 1]
                    place, count = 2 * ny + (0 if o[1] > 0 else nx), nx
                else:
                    source = qs.at[slot, pl.ds(x_row + y_row, 1), :]
                    place = face_rows + (0 if o[0] > 0 else 2) + (0 if o[1] > 0 else 1)
                    count = 1
                remote(source, recvf.at[slot, pl.ds(place, count), :], send, recv, o).start()

    def halo_start(value, slot):
        halo_pack(value, slot)
        halo_send(slot)

    def halo_finish(slot):
        drain(recvf.at[slot], rxy.at[slot])
        drain(recvz.at[slot], rzs.at[slot, 1])
        for h in range(halves):
            piece = slice(h * LANES, (h + 1) * LANES)
            arrived = recvz[slot, pl.ds(h, 18, stride=halves), :] * zmask[:, piece]
            low = jnp.sum(arrived[0:9], axis=0, keepdims=True)
            high = jnp.sum(arrived[9:18], axis=0, keepdims=True)
            pair = jnp.concatenate([low, high, jnp.zeros((6, LANES), jnp.float32)], axis=0)
            down = jnp.transpose(pair)
            at_ends = jnp.where(lane == 0, down[:, 0:1], jnp.where(lane == nz - 1, down[:, 1:2], 0.0))
            az[piece, :] = qs[slot, piece, :] + at_ends
        faces = recvf.at[slot]
        az[0:ny, :] += faces[0:ny, :] * has_lo[0]
        az[rows - ny : rows, :] += faces[ny : 2 * ny, :] * has_hi[0]
        az[pl.ds(0, nx, stride=ny), :] += faces[2 * ny : 2 * ny + nx, :] * has_lo[1]
        az[pl.ds(ny - 1, nx, stride=ny), :] += faces[2 * ny + nx : face_rows, :] * has_hi[1]
        corners = (
            (0, has_lo[0] * has_lo[1]),
            (ny - 1, has_lo[0] * has_hi[1]),
            (rows - ny, has_hi[0] * has_lo[1]),
            (rows - 1, has_hi[0] * has_hi[1]),
        )
        for n, (place, flag) in enumerate(corners):
            az[place : place + 1, :] += faces[face_rows + n : face_rows + n + 1, :] * flag
        drain(recvf.at[slot], sxy.at[slot])
        drain(recvz.at[slot], rzs.at[slot, 0])
        return az[...]

    mrows = crows + 1

    def plane_start(par):
        for n, o in enumerate(plane_peers):
            remote(
                msg.at[par, 0, pl.ds(0, mrows), :], arp.at[par, n], ssa.at[par, 0], rpa.at[par], o
            ).start()

    def sum_of_row():
        own = pl.ds(crows, 1)
        for n, o in enumerate(plane_peers):
            place = arps.at[pl.ds(n, 1), :]
            remote(msg.at[1, 0, own, :], place, ssa.at[2, 0], rpa.at[2], o).start()
        drain(arps, rpa.at[2])
        here = msg[1, 0, crows : crows + 1] + jnp.sum(arps[...], axis=0, keepdims=True)
        msg[1, 1, crows : crows + 1] = here
        for n, o in enumerate(line_peers):
            place = arzs.at[pl.ds(n, 1), :]
            remote(msg.at[1, 1, own, :], place, ssa.at[2, 1], rza.at[2], o).start()
        drain(arzs, rza.at[2])
        drain(arps, ssa.at[2, 0])
        drain(arzs, ssa.at[2, 1])
        return here + jnp.sum(arzs[...], axis=0, keepdims=True)

    def plane_finish_line_start(par):
        drain(arp.at[par], rpa.at[par])
        msg[par, 1, 0:mrows] = msg[par, 0, 0:mrows] + jnp.sum(arp[par], axis=0)
        for n, o in enumerate(line_peers):
            remote(
                msg.at[par, 1, pl.ds(0, mrows), :], arz.at[par, n], ssa.at[par, 1], rza.at[par], o
            ).start()

    def line_finish(par):
        drain(arz.at[par], rza.at[par])
        total = msg[par, 1, 0:mrows] + jnp.sum(arz[par], axis=0)
        drain(arp.at[par], ssa.at[par, 0])
        drain(arz.at[par], ssa.at[par, 1])
        return total

    def grad(value):
        gxy = left_product(lxh[...], lxl[...], value)
        return gxy, right_product(value, rzb[...], rzh[...])

    def grad_transposed(wxy, wz):
        return left_product(lth[...], ltl[...], wxy) + right_product(wz, rtb[...], rth[...])

    def twice(value):
        return jnp.concatenate([value, value], axis=0)

    def total_of(value):
        return jnp.sum(jnp.sum(value, axis=0, keepdims=True), axis=1, keepdims=True)

    def spread(coarse):
        acc = jnp.zeros((16, nz), jnp.float32)
        for kz in range(3):
            product = xnb[kz, :, 0:LANES] * coarse[0:1, :]
            for j in range(1, crows):
                product = product + xnb[kz, :, j * LANES : (j + 1) * LANES] * coarse[j : j + 1, :]
            acc = acc + jnp.sum(product, axis=1, keepdims=True) * phi_z[kz]
        high, low = parts_of(acc)
        rest = (acc - high.astype(jnp.float32) - low.astype(jnp.float32)).astype(jnp.bfloat16)
        return mm(phit[...], jnp.concatenate([high, low, rest], axis=0))

    for n in (0, 4, 5, 8, 9, 1):
        loads[n].wait()
    level = ls[...]
    gxy, gz = grad(level)
    advect = vel[0] * gxy[0:rows] + vel[1] * gxy[rows:] + vel[2] * gz
    b = mass[...]
    halo_pack(b * advect, 0)
    for n in (2, 6, 7, 10, 11):
        loads[n].wait()
    halo_pack(
        grad_transposed(jnp.concatenate([b * vel[0], b * vel[1]], axis=0), b * vel[2])
        + b * src[...],
        1,
    )
    pl.semaphore_wait(barrier, len(peers))
    halo_send(0)
    halo_send(1)
    for o in OFFSETS:
        place = pl.ds(OFFSETS.index(o) * crows, crows)
        remote(xrow, xin.at[place, :], xss.at[0], xrs.at[0], o).start()
    level = level - TIME_STEP * halo_finish(0) * ibw[...]
    for sweep in range(RSWEEPS):
        gxy, gz = grad(level)
        gx, gy = gxy[0:rows], gxy[rows:]
        inv_norm = lax.rsqrt(1.0 + gx * gx + gy * gy + gz * gz)
        factor = mass[...] * (level * (1.0 - level) * inv_norm - INTERFACE_WIDTH)
        slot = (2 + sweep) % 3
        halo_start(grad_transposed(twice(factor) * gxy, factor * gz), slot)
        if sweep == 0:
            rhs = SOURCE_SCALE * halo_finish(1)
            rf[...] = rhs
            restricted = total_of(wt[...] * rhs)
            for j in range(crows):
                msg[1, 0, j : j + 1, :] = restricted * xrow[j : j + 1, :]
            plane_start(1)
        else:
            plane_finish_line_start(1)
        level = level + PSEUDO_STEP * halo_finish(slot) * ibw[...]
    lev_out[...] = level
    level_copy = pltpu.make_async_copy(lev_out, lev_hbm, osem.at[0])
    level_copy.start()

    b = mass[...]
    sc = b / (GAS_DENSITY + (1.0 - GAS_DENSITY) * jnp.clip(level, 0.0, 1.0))
    scaled[...] = sc
    for n in (12, 13):
        loads[n].wait()
    halo_start(
        left_product(sqb[0], sqb[1], sc) + right_product(sc, szb[...], szb[:, 0:nz]) + b, 1
    )
    coarse = line_finish(1)
    mv[0, 0:crows] = coarse[0:crows]
    drain(xin, xrs.at[0])
    drain(xin, xss.at[0])
    for n, o in enumerate(OFFSETS):
        for j in range(crows):
            xnb[1 - o[2], nine(o) : nine(o) + 1, j * LANES : (j + 1) * LANES] = xin[
                n * crows + j : n * crows + j + 1, :
            ]
    spread_now = spread(coarse)
    inverse = 1.0 / halo_finish(1)
    invd[...] = inverse
    zf[...] = rf[...] * inverse + spread_now

    def element_operator(value):
        gxy, gz = grad(value)
        sc = scaled[...]
        return grad_transposed(twice(sc) * gxy, sc * gz) + mass[...] * value

    lane1 = lax.broadcasted_iota(jnp.int32, (1, LANES), 1)

    def send_sums(par, z, q):
        inner = total_of(wt[...] * rf[...] * z)
        energy = total_of(q * z)
        cross = total_of(q * pf[...])
        msg[par, 0, crows : crows + 1, :] = jnp.where(
            lane1 == 0, inner, jnp.where(lane1 == 1, energy, jnp.where(lane1 == 2, cross, 0.0))
        )

    def steps_from(sums, step):
        inner, energy, cross = sums[:, 0:1], sums[:, 1:2], sums[:, 2:3]
        old_inner, old_curve = mv[2, 0:1, 0:1], mv[2, 1:2, 0:1]
        ratio = jnp.where(step > 0, inner / old_inner, 0.0)
        curve = energy + 2.0 * ratio * cross + ratio * ratio * old_curve
        return inner, ratio, curve, inner / curve

    mv[2] = jnp.ones((8, LANES), jnp.float32)

    def iteration(step, carry):
        slot = lax.rem(step, 2)
        z = zf[...]
        q = element_operator(z)
        high, low = parts_of(q)
        wide = mm(phi[...].astype(jnp.bfloat16), jnp.concatenate([high, low], axis=1))
        tested = wide[:, :nz] + wide[:, nz:]
        columns = [jnp.sum(tested * phi_z[kz], axis=1, keepdims=True) for kz in range(3)]
        for j in range(crows):
            part = columns[0] * xnb[0, :, j * LANES : (j + 1) * LANES]
            for kz in (1, 2):
                part = part + columns[kz] * xnb[kz, :, j * LANES : (j + 1) * LANES]
            msg[slot, 0, j : j + 1, :] = jnp.sum(part, axis=0, keepdims=True)
        send_sums(slot, z, q)
        plane_start(slot)
        halo_start(q, slot)
        plane_finish_line_start(slot)
        p_out[...] += mv[2, 2:3, 0:1] * pf[...]
        az_now = halo_finish(slot)
        total = line_finish(slot)
        inner, ratio, curve, size = steps_from(total[crows : crows + 1, :], step)
        coarse_step = total[0:crows] + ratio * mv[1, 0:crows]
        coarse = mv[0, 0:crows] - size * coarse_step
        mv[1, 0:crows] = coarse_step
        mv[0, 0:crows] = coarse
        ap = az_now + ratio * apf[...]
        r = rf[...] - size * ap
        apf[...] = ap
        rf[...] = r
        pf[...] = z + ratio * pf[...]
        mv[2, 2:3, :] = jnp.broadcast_to(size, (1, LANES))
        mv[2, 0:1, :] = jnp.broadcast_to(inner, (1, LANES))
        mv[2, 1:2, :] = jnp.broadcast_to(curve, (1, LANES))
        zf[...] = r * invd[...] + spread(coarse)
        return carry

    lax.fori_loop(0, ITERS - 1, iteration, 0)

    z = zf[...]
    send_sums(1, z, element_operator(z))
    _, ratio, _, size = steps_from(sum_of_row(), ITERS - 1)
    p_out[...] = (p_out[...] + mv[2, 2:3, 0:1] * pf[...]) + size * (z + ratio * pf[...])
    pressure_copy = pltpu.make_async_copy(p_out, p_hbm, osem.at[1])
    pressure_copy.start()
    level_copy.wait()
    pressure_copy.wait()


def body(sizes, level_set, velocity, source, coarse_factor):
    nx, ny, nz = level_set.shape
    rows = nx * ny
    ncoarse = coarse_factor.shape[1]
    crows = ncoarse // LANES
    tables = block_tables(nx, ny, nz)
    sx, sy, sz = sizes
    f32 = jnp.float32

    def vm(*shape):
        return pltpu.VMEM(shape, f32)

    dma = pltpu.SemaphoreType.DMA
    face_rows = 2 * ny + 2 * nx
    halves = rows // LANES
    operands = [
        level_set.reshape(rows, nz),
        velocity.reshape(3, rows, nz),
        source.reshape(rows, nz),
        coarse_factor.reshape(crows, LANES),
        *[jnp.asarray(t) for t in tables],
    ]
    scratch = [pltpu.VMEM(a.shape, a.dtype) for a in operands] + [
        vm(3, rows, nz),
        vm(3, 2, nx, nz),
        vm(3, 9, 2 * halves, LANES),
        vm(3, face_rows + 4, nz),
        vm(3, 18 * halves, LANES),
        vm(rows, nz),
        vm(2, 2, 8, LANES),
        vm(2, sx * sy - 1, crows + 1, LANES),
        vm(2, sz - 1, crows + 1, LANES),
        vm(3, 16, ncoarse),
        vm(len(OFFSETS) * crows, LANES),
        vm(18, rows),
        vm(16, rows),
        vm(rows, nz),
        vm(rows, nz),
        vm(rows, nz),
        vm(rows, nz),
        vm(rows, nz),
        vm(rows, nz),
        vm(rows, nz),
        vm(rows, nz),
        vm(3, 8, LANES),
        dma((3,)),
        dma((3,)),
        dma((3, 2)),
        dma((3, 2)),
        dma((3,)),
        dma((3,)),
        dma((1,)),
        dma((1,)),
        vm(sx * sy - 1, LANES),
        vm(sz - 1, LANES),
        pltpu.VMEM((rows, 48), jnp.bfloat16),
        dma((len(operands),)),
        vm(rows, nz),
        vm(rows, nz),
        dma((2,)),
    ]
    level, pressure = pl.pallas_call(
        functools.partial(kernel, (sizes, nx, ny, nz, ncoarse)),
        out_shape=(jax.ShapeDtypeStruct((rows, nz), f32),) * 2,
        in_specs=[pl.BlockSpec(memory_space=pltpu.HBM)] * len(operands),
        out_specs=(pl.BlockSpec(memory_space=pltpu.HBM),) * 2,
        scratch_shapes=scratch,
        compiler_params=pltpu.CompilerParams(
            collective_id=0, has_side_effects=True, vmem_limit_bytes=63 * 1024 * 1024
        ),
        name="transport_and_pressure",
    )(*operands)
    return level.reshape(nx, ny, nz), pressure.reshape(nx, ny, nz)


def solution(mesh):
    sizes = tuple(mesh.shape[a] for a in AXES)
    in_specs = (
        P("gx", "gy", "gz"),
        P(None, "gx", "gy", "gz"),
        P("gx", "gy", "gz"),
        P(("gx", "gy", "gz"), None),
    )
    out_specs = (P("gx", "gy", "gz"), P("gx", "gy", "gz"))
    return jax.shard_map(
        functools.partial(body, sizes),
        mesh=mesh,
        in_specs=in_specs,
        out_specs=out_specs,
        check_vma=False,
    )
```
